32 devices in a mesh: dp: 4 (over z), seq: 8 (over y, x, core).
Axes of the slice: x: 2, y: 2, z: 4, core: 2. Of those that a mesh axis runs over, the one named last changes fastest.
Arguments:
- block_input: bfloat16 [8, 1024, 768], P('dp', 'seq'), may hold values from -6 to 6
- qkv_weight: bfloat16 [1769472], P(('dp', 'seq')), may hold values from -2.020726 to 2.020726
- proj_weight: bfloat16 [589824], P(('dp', 'seq')), may hold values from -0.875 to 0.875
- up_weight: bfloat16 [2359296], P(('dp', 'seq')), may hold values from -0.21875 to 0.21875
- down_weight: bfloat16 [2359296], P(('dp', 'seq')), may hold values from -0.109375 to 0.109375
- vectors: bfloat16 [9216], P(('dp', 'seq')), may hold values from -1 to 1.5
- out_grad: bfloat16 [8, 1024, 768], P('dp', 'seq'), may hold values from -6 to 6
Outputs:
- block_output: bfloat16 [8, 1024, 768], P('dp', 'seq')
- input_grad: bfloat16 [8, 1024, 768], P('dp', 'seq')
- qkv_grad: float32 [1769472], P(('dp', 'seq'))
- proj_grad: float32 [589824], P(('dp', 'seq'))
- up_grad: float32 [2359296], P(('dp', 'seq'))
- down_grad: float32 [2359296], P(('dp', 'seq'))
- vector_grad: float32 [9216], P(('dp', 'seq'))
The draws below stay inside these ranges and needn't reach their ends.
All inputs are finite; a program needn't handle non-finite values.
Results may differ from the reference program's by a relative error of at most 0.012.
The reference program's roundings to bfloat16 on the way count: a program that leaves them out, or rounds other values in their place, can miss the bound.
Values may be sent and summed in bfloat16 or wider, within the bound.
No kernel may reach another device: no remote copies, remote signals or barrier semaphores. Data moves between devices by JAX's collectives and lax.ppermute only.
A program may use at most 192 MiB of HBM per device.

```python
import jax
import jax.numpy as jnp
from jax import lax

D = 768
H = 12
FF = 3072
LEN = 1024
BATCH = 8


def draw_block_input(key, part):
    return jnp.clip(jax.random.normal(key, (BATCH, LEN, D), jnp.float32), -6.0, 6.0).astype(jnp.bfloat16)


def draw_qkv_weight(key, part):
    spread = D ** (-0.5)
    return (jnp.clip(jax.random.normal(key, (D * 3 * D,), jnp.float32), -6.0, 6.0) * spread).astype(jnp.bfloat16)


def draw_vectors(key, part):
    total_len = 8 * D + FF
    positions = jnp.arange(total_len)
    gain_mask = (positions < D) | (positions >= 5 * D) & (positions < 6 * D)
    gains = 0.6 + 0.8 * jax.random.uniform(key, (total_len,), jnp.float32)
    biases = jnp.clip(0.3 * jax.random.normal(jax.random.fold_in(key, 5), (total_len,), jnp.float32), -1.0, 1.0)
    return jnp.where(gain_mask, gains, biases).astype(jnp.bfloat16)


def level_of(key, shape, pieces, least, top_value):
    factor_of = 1.0
    for axis_at, shards_of in pieces:
        heights = jax.random.uniform(jax.random.fold_in(jax.random.fold_in(key, 6), axis_at), (shards_of,), jnp.float32, least / len(pieces), top_value / len(pieces))
        factor_of = factor_of * jnp.repeat(jnp.exp(heights), shape[axis_at] // shards_of).reshape((-1,) + (1,) * (len(shape) - 1 - axis_at))
    return factor_of


def noise(own_key, shape, scale, most, split=(), kind=jnp.bfloat16):
    level = level_of(own_key, shape, split, -0.22, 0.18) if split else 1.0
    values = jax.random.normal(own_key, shape, jnp.float32) * scale * level
    return jnp.minimum(jnp.maximum(values, -most), most).astype(kind)


def setup_inputs(seed: int = 0) -> dict:
    seeds = jax.random.split(jax.random.key(seed), 8)
    return {
        "block_input": draw_block_input(jax.random.fold_in(seeds[7], 71), 0),
        "qkv_weight": draw_qkv_weight(jax.random.fold_in(seeds[7], 71), 0),
        "proj_weight": noise(seeds[2], (D * D,), (D // 16) ** -0.5, 0.875, ((0, 32),)),
        "up_weight": noise(seeds[3], (D * FF,), D ** -0.5, 0.21875, ((0, 32),)),
        "down_weight": noise(seeds[4], (FF * D,), FF ** -0.5, 0.109375, ((0, 32),)),
        "vectors": draw_vectors(jax.random.fold_in(seeds[7], 71), 0),
        "out_grad": noise(seeds[6], (BATCH, LEN, D), 1.0, 6.0, ((0, 4), (1, 8))),
    }


norm_eps = 1e-05
gelu_coeff = 0.7978845608028654
cubic_coeff = 0.044715
highest = lax.Precision.HIGHEST

@jax.custom_vjp
def low(v):
    return lax.optimization_barrier(v.astype(jnp.bfloat16)).astype(jnp.float32)

@jax.custom_vjp
def low_back(v):
    return v

def low_keep(v):
    return (low(v), None)

def low_pass(kept, grad):
    return (grad,)

def back_keep(v):
    return (v, None)

def back_low(kept, grad):
    return (low(grad),)
low.defvjp(low_keep, low_pass)
low_back.defvjp(back_keep, back_low)

def layer_normalize(values, gain_vec, shift_vec):
    center = values - lax.optimization_barrier(jnp.mean(values, axis=-1, keepdims=True))
    inverse = lax.rsqrt(lax.optimization_barrier(jnp.mean(center * center, axis=-1, keepdims=True)) + norm_eps)
    return center * inverse * gain_vec + shift_vec

def gelu_tanh(pre_act):
    return 0.5 * pre_act * (1.0 + jnp.tanh(gelu_coeff * (pre_act + cubic_coeff * pre_act * pre_act * pre_act)))

def split_vectors(vectors):
    offsets = [0, D, 2 * D, 3 * D, 4 * D, 5 * D, 6 * D, 7 * D, 7 * D + FF, 8 * D + FF]
    return [vectors[offsets[number]:offsets[number + 1]] for number in range(9)]

def attention(queries, all_keys, all_values):
    length = queries.shape[0]
    query_block = min(512, length)
    head_size = D // H
    scaling = head_size ** (-0.5)
    q_blocks = queries.reshape(length // query_block, query_block, H, head_size)
    starts = jnp.arange(length // query_block, dtype=jnp.int32) * query_block
    key_pos = jnp.arange(length, dtype=jnp.int32)

    def one_block(element):
        q_block, start_row = element
        raw_scores = jnp.einsum('qhd,khd->hqk', q_block, all_keys, precision=highest) * scaling
        query_pos = start_row + jnp.arange(query_block, dtype=jnp.int32)
        allowed = query_pos[:, None] >= key_pos[None, :]
        scores = low_back(jnp.where(allowed[None], raw_scores, -1e+30))
        row_max = lax.optimization_barrier(jnp.max(scores, axis=-1, keepdims=True))
        expo = jnp.exp(scores - row_max)
        probs = low(expo / lax.optimization_barrier(jnp.sum(expo, axis=-1, keepdims=True)))
        return jnp.einsum('hqk,khd->qhd', probs, all_values, precision=highest)
    attended = lax.map(jax.checkpoint(one_block), (q_blocks, starts))
    return attended.reshape(length, D)

def forward(input_tokens, qkv_weight, proj_weight, up_weight, down_weight, vectors):
    first_norm_gain, first_norm_bias, query_bias, value_bias, proj_bias, second_norm_gain, second_norm_bias, up_bias, down_bias = split_vectors(vectors)
    length = input_tokens.shape[0]
    head_size = D // H
    act_one = low(layer_normalize(input_tokens, first_norm_gain, first_norm_bias))
    mixed = jnp.dot(act_one, qkv_weight.reshape(D, 3 * D), precision=highest, preferred_element_type=jnp.float32)
    queries = low_back(low(mixed[:, :D] + query_bias))
    all_keys = low_back(low(mixed[:, D:2 * D]))
    all_values = low_back(low(mixed[:, 2 * D:] + value_bias))
    attended = attention(queries.reshape(length, H, head_size), all_keys.reshape(length, H, head_size), all_values.reshape(length, H, head_size))
    act_two = low_back(low(attended))
    branch_one = low_back(jnp.dot(act_two, proj_weight.reshape(D, D), precision=highest, preferred_element_type=jnp.float32) + proj_bias)
    residual_midpoint = input_tokens + branch_one
    act_three = low(layer_normalize(residual_midpoint, second_norm_gain, second_norm_bias))
    pre_act = low_back(jnp.dot(act_three, up_weight.reshape(D, FF), precision=highest, preferred_element_type=jnp.float32) + up_bias)
    act_four = low(gelu_tanh(pre_act))
    branch_two = low_back(jnp.dot(act_four, down_weight.reshape(FF, D), precision=highest, preferred_element_type=jnp.float32) + down_bias)
    return residual_midpoint + branch_two

def reference(block_input, qkv_weight, proj_weight, up_weight, down_weight, vectors, out_grad):
    params = tuple((weight.astype(jnp.float32) for weight in (qkv_weight, proj_weight, up_weight, down_weight, vectors)))

    def one_sequence(running, element):
        seq_in, seq_grad = element
        result, pull_back = jax.vjp(forward, seq_in.astype(jnp.float32), *params)
        grad_all = pull_back(seq_grad.astype(jnp.float32))
        running = tuple((acc_now + grad_now for acc_now, grad_now in zip(running, grad_all[1:])))
        return (running, (result.astype(jnp.bfloat16), grad_all[0].astype(jnp.bfloat16)))
    starting = tuple((jnp.zeros(param.shape, jnp.float32) for param in params))
    totals, (outputs, in_grads) = lax.scan(one_sequence, starting, (block_input, out_grad))
    return (outputs, in_grads, totals[0], totals[1], totals[2], totals[3], totals[4])
```

```python
import jax
import jax.numpy as jnp
from jax import lax
from jax.sharding import PartitionSpec as P

H = 12


norm_eps = 1e-05
gelu_coeff = 0.7978845608028654
cubic_coeff = 0.044715
masked_value = -1e30


def layer_normalize(values, gain_vec, shift_vec):
    center = values - jnp.mean(values, axis=-1, keepdims=True)
    inverse = lax.rsqrt(jnp.mean(center * center, axis=-1, keepdims=True) + norm_eps)
    normed = center * inverse
    return (normed * gain_vec + shift_vec, normed, inverse)


def norm_back(grad_norm, normed, inverse, gain_vec):
    scaled = grad_norm * gain_vec
    inner_part = (
        scaled
        - jnp.mean(scaled, axis=-1, keepdims=True)
        - normed * jnp.mean(scaled * normed, axis=-1, keepdims=True)
    )
    return (inverse * inner_part, jnp.sum(grad_norm * normed, axis=0), jnp.sum(grad_norm, axis=0))


def gelu_both(pre_act):
    cubic = pre_act + cubic_coeff * pre_act * pre_act * pre_act
    tanh_part = jnp.tanh(gelu_coeff * cubic)
    value_now = 0.5 * pre_act * (1.0 + tanh_part)
    slope = 0.5 * (1.0 + tanh_part) + 0.5 * pre_act * (1.0 - tanh_part * tanh_part) * gelu_coeff * (
        1.0 + 3.0 * cubic_coeff * pre_act * pre_act
    )
    return (value_now, slope)


def split_vectors(vectors, model_width, hidden_width):
    offsets = [
        0,
        model_width,
        2 * model_width,
        3 * model_width,
        4 * model_width,
        5 * model_width,
        6 * model_width,
        7 * model_width,
        7 * model_width + hidden_width,
        8 * model_width + hidden_width,
    ]
    return tuple((vectors[offsets[number] : offsets[number + 1]] for number in range(9)))


def block_scores(queries, all_keys, all_values, key_index, key_block, first_query, scaling):
    start_row = key_index * key_block
    key_part = lax.dynamic_slice_in_dim(all_keys, start_row, key_block, 0)
    value_part = lax.dynamic_slice_in_dim(all_values, start_row, key_block, 0)
    raw_scores = (
        jnp.einsum("qhd,khd->hqk", queries, key_part, preferred_element_type=jnp.float32) * scaling
    )
    query_pos = first_query + lax.broadcasted_iota(jnp.int32, (queries.shape[0], key_block), 0)
    key_pos = start_row + lax.broadcasted_iota(jnp.int32, (queries.shape[0], key_block), 1)
    return (jnp.where((key_pos <= query_pos)[None], raw_scores, masked_value), key_part, value_part)


def attend(queries, all_keys, all_values, first_query):
    row_count, head_count, head_size = queries.shape
    key_block = min(512, all_keys.shape[0])
    scaling = head_size ** (-0.5)
    block_count = (first_query + row_count - 1) // key_block + 1

    def statistics(key_index, running):
        row_max, row_sum = running
        scores = block_scores(
            queries, all_keys, all_values, key_index, key_block, first_query, scaling
        )[0]
        new_max = jnp.maximum(row_max, jnp.max(scores, axis=-1))
        row_sum = row_sum * jnp.exp(row_max - new_max) + jnp.sum(
            jnp.exp(scores - new_max[:, :, None]), axis=-1
        )
        return (new_max, row_sum)

    starting = (
        jnp.full((head_count, row_count), masked_value, jnp.float32),
        jnp.zeros((head_count, row_count), jnp.float32),
    )
    row_max, row_sum = lax.fori_loop(0, block_count, statistics, starting)
    log_norm = row_max + jnp.log(row_sum)

    def accumulate(key_index, running):
        att_out, exact_out = running
        scores, key_part, value_part = block_scores(
            queries, all_keys, all_values, key_index, key_block, first_query, scaling
        )
        prob_exact = jnp.exp(scores - log_norm[:, :, None])
        prob_block = prob_exact.astype(jnp.bfloat16)
        att_out = att_out + jnp.einsum(
            "hqk,khd->qhd", prob_block, value_part, preferred_element_type=jnp.float32
        )
        exact_out = exact_out + jnp.einsum(
            "hqk,khd->qhd",
            prob_exact,
            value_part.astype(jnp.float32),
            precision=lax.Precision.HIGHEST,
            preferred_element_type=jnp.float32,
        )
        return (att_out, exact_out)

    zeros_out = jnp.zeros((row_count, head_count, head_size), jnp.float32)
    att_out, exact_out = lax.fori_loop(0, block_count, accumulate, (zeros_out, zeros_out))
    return (att_out, exact_out, log_norm)


def attend_back(queries, all_keys, all_values, first_query, grad_out, exact_out, log_norm):
    row_count, head_count, head_size = queries.shape
    key_block = min(512, all_keys.shape[0])
    scaling = head_size ** (-0.5)
    block_count = (first_query + row_count - 1) // key_block + 1
    row_dot = jnp.einsum("qhd,qhd->hq", grad_out.astype(jnp.float32), exact_out)

    def one_block(key_index, running):
        grad_query, grad_keys, grad_values = running
        scores, key_part, value_part = block_scores(
            queries, all_keys, all_values, key_index, key_block, first_query, scaling
        )
        prob_block = jnp.exp(scores - log_norm[:, :, None])
        value_grad = jnp.einsum(
            "hqk,qhd->khd",
            prob_block.astype(jnp.bfloat16),
            grad_out,
            preferred_element_type=jnp.float32,
        )
        prob_grad = jnp.einsum(
            "qhd,khd->hqk", grad_out, value_part, preferred_element_type=jnp.float32
        )
        score_grad = (prob_block * (prob_grad - row_dot[:, :, None])).astype(jnp.bfloat16)
        grad_query = (
            grad_query
            + jnp.einsum("hqk,khd->qhd", score_grad, key_part, preferred_element_type=jnp.float32)
            * scaling
        )
        key_grad = (
            jnp.einsum("hqk,qhd->khd", score_grad, queries, preferred_element_type=jnp.float32)
            * scaling
        )
        start_row = key_index * key_block
        grad_keys = lax.dynamic_update_slice_in_dim(grad_keys, key_grad, start_row, 0)
        grad_values = lax.dynamic_update_slice_in_dim(grad_values, value_grad, start_row, 0)
        return (grad_query, grad_keys, grad_values)

    starting = (
        jnp.zeros((row_count, head_count, head_size), jnp.float32),
        jnp.zeros(all_keys.shape, jnp.float32),
        jnp.zeros(all_values.shape, jnp.float32),
    )
    return lax.fori_loop(0, block_count, one_block, starting)


def local(block_input, qkv_weight, proj_weight, up_weight, down_weight, vectors, out_grad):
    seq_count, row_count, model_width = block_input.shape
    token_count = seq_count * row_count
    head_count = H
    head_size = model_width // head_count
    first_query = lax.axis_index("seq") * row_count
    gathered = (
        lax.all_gather(qkv_weight, ("dp", "seq"), axis=0, tiled=True),
        lax.all_gather(proj_weight, ("dp", "seq"), axis=0, tiled=True),
        lax.all_gather(up_weight, ("dp", "seq"), axis=0, tiled=True),
        lax.all_gather(down_weight, ("dp", "seq"), axis=0, tiled=True),
        lax.all_gather(vectors, ("dp", "seq"), axis=0, tiled=True),
    )
    hidden_width = gathered[2].shape[0] // model_width

    def unpack(pieces):
        return (
            pieces[0].reshape(model_width, 3 * model_width),
            pieces[1].reshape(model_width, model_width),
            pieces[2].reshape(model_width, hidden_width),
            pieces[3].reshape(hidden_width, model_width),
            split_vectors(pieces[4].astype(jnp.float32), model_width, hidden_width),
        )

    mat_qkv, mat_proj, mat_up, mat_down, vec_parts = unpack(gathered)
    (
        first_norm_gain,
        first_norm_bias,
        query_bias,
        value_bias,
        proj_bias,
        second_norm_gain,
        second_norm_bias,
        up_bias,
        down_bias,
    ) = vec_parts
    input_tokens = block_input.reshape(token_count, model_width).astype(jnp.float32)
    first_normed_rows, first_centered_scaled, first_inverse_deviation = layer_normalize(
        input_tokens, first_norm_gain, first_norm_bias
    )
    act_one = first_normed_rows.astype(jnp.bfloat16)
    mixed = jnp.dot(act_one, mat_qkv, preferred_element_type=jnp.float32)
    shape_four = (seq_count, row_count, head_count, head_size)
    q_four = (mixed[:, :model_width] + query_bias).astype(jnp.bfloat16).reshape(shape_four)
    k_four = mixed[:, model_width : 2 * model_width].astype(jnp.bfloat16).reshape(shape_four)
    v_four = (mixed[:, 2 * model_width :] + value_bias).astype(jnp.bfloat16).reshape(shape_four)

    def forward_one(running, element):
        query_seq, key_seq, value_seq = element
        all_keys, all_values = (
            lax.all_gather(key_seq, "seq", axis=0, tiled=True),
            lax.all_gather(value_seq, "seq", axis=0, tiled=True),
        )
        att_out, exact_out, log_norm = attend(query_seq, all_keys, all_values, first_query)
        return (running, (att_out, exact_out, log_norm))

    unused_fwd, (att_all, exact_all, norm_all) = lax.scan(
        forward_one, None, (q_four, k_four, v_four)
    )
    act_two = att_all.reshape(token_count, model_width).astype(jnp.bfloat16)
    residual_midpoint = (
        input_tokens + jnp.dot(act_two, mat_proj, preferred_element_type=jnp.float32) + proj_bias
    )
    second_normed_rows, second_centered_scaled, second_inverse_deviation = layer_normalize(
        residual_midpoint, second_norm_gain, second_norm_bias
    )
    act_three = second_normed_rows.astype(jnp.bfloat16)
    pre_act = jnp.dot(act_three, mat_up, preferred_element_type=jnp.float32) + up_bias
    activated, slope = gelu_both(pre_act)
    act_four = activated.astype(jnp.bfloat16)
    result = (
        residual_midpoint
        + jnp.dot(act_four, mat_down, preferred_element_type=jnp.float32)
        + down_bias
    )
    block_output = result.astype(jnp.bfloat16).reshape(seq_count, row_count, model_width)
    back_weights = unpack(
        (
            lax.all_gather(qkv_weight, ("dp", "seq"), axis=0, tiled=True),
            lax.all_gather(proj_weight, ("dp", "seq"), axis=0, tiled=True),
            lax.all_gather(up_weight, ("dp", "seq"), axis=0, tiled=True),
            lax.all_gather(down_weight, ("dp", "seq"), axis=0, tiled=True),
            lax.all_gather(vectors, ("dp", "seq"), axis=0, tiled=True),
        )
    )
    back_qkv, back_proj, back_up, back_down, back_vec = back_weights
    backward_first_gain = back_vec[0]
    backward_second_gain = back_vec[5]
    grad_top = out_grad.reshape(token_count, model_width)
    grad_top_f = grad_top.astype(jnp.float32)
    down_grad = jnp.dot(act_four.T, grad_top, preferred_element_type=jnp.float32)
    down_bias_grad = jnp.sum(grad_top_f, axis=0)
    grad_act = jnp.dot(grad_top, back_down.T, preferred_element_type=jnp.float32)
    grad_pre = (grad_act * slope).astype(jnp.bfloat16)
    up_grad = jnp.dot(act_three.T, grad_pre, preferred_element_type=jnp.float32)
    up_bias_grad = jnp.sum(grad_pre.astype(jnp.float32), axis=0)
    second_norm_gradient = jnp.dot(grad_pre, back_up.T, preferred_element_type=jnp.float32)
    grad_mid_part, gain_two_grad, shift_two_grad = norm_back(
        second_norm_gradient, second_centered_scaled, second_inverse_deviation, backward_second_gain
    )
    grad_middle = grad_top_f + grad_mid_part
    up_sum, down_sum = (
        lax.psum_scatter(up_grad.reshape(-1), ("dp", "seq"), scatter_dimension=0, tiled=True),
        lax.psum_scatter(down_grad.reshape(-1), ("dp", "seq"), scatter_dimension=0, tiled=True),
    )
    grad_branch = grad_middle.astype(jnp.bfloat16)
    proj_grad = jnp.dot(act_two.T, grad_branch, preferred_element_type=jnp.float32)
    proj_bias_grad = jnp.sum(grad_branch.astype(jnp.float32), axis=0)
    grad_att = jnp.dot(grad_branch, back_proj.T, preferred_element_type=jnp.float32).astype(
        jnp.bfloat16
    )

    def backward_one(running, element):
        query_seq, key_seq, value_seq, grad_seq, exact_seq, norm_seq = element
        all_keys, all_values = (
            lax.all_gather(key_seq, "seq", axis=0, tiled=True),
            lax.all_gather(value_seq, "seq", axis=0, tiled=True),
        )
        grad_query, grad_keys, grad_values = attend_back(
            query_seq, all_keys, all_values, first_query, grad_seq, exact_seq, norm_seq
        )
        key_part, value_part = (
            lax.psum_scatter(
                grad_keys.astype(jnp.bfloat16), "seq", scatter_dimension=0, tiled=True
            ).astype(jnp.float32),
            lax.psum_scatter(
                grad_values.astype(jnp.bfloat16), "seq", scatter_dimension=0, tiled=True
            ).astype(jnp.float32),
        )
        return (
            running,
            (
                grad_query.astype(jnp.bfloat16),
                key_part.astype(jnp.bfloat16),
                value_part.astype(jnp.bfloat16),
            ),
        )

    unused_back, (grad_q_four, grad_k_four, grad_v_four) = lax.scan(
        backward_one,
        None,
        (q_four, k_four, v_four, grad_att.reshape(shape_four), exact_all, norm_all),
    )
    grad_queries = grad_q_four.reshape(token_count, model_width)
    grad_values_all = grad_v_four.reshape(token_count, model_width)
    grad_mixed = jnp.concatenate(
        [grad_queries, grad_k_four.reshape(token_count, model_width), grad_values_all], axis=1
    )
    qkv_grad = jnp.dot(act_one.T, grad_mixed, preferred_element_type=jnp.float32)
    query_bias_grad = jnp.sum(grad_queries.astype(jnp.float32), axis=0)
    value_bias_grad = jnp.sum(grad_values_all.astype(jnp.float32), axis=0)
    first_norm_gradient = jnp.dot(grad_mixed, back_qkv.T, preferred_element_type=jnp.float32)
    grad_in_part, gain_one_grad, shift_one_grad = norm_back(
        first_norm_gradient, first_centered_scaled, first_inverse_deviation, backward_first_gain
    )
    input_grad = (
        (grad_middle + grad_in_part).astype(jnp.bfloat16).reshape(seq_count, row_count, model_width)
    )
    vector_grad = jnp.concatenate(
        [
            gain_one_grad,
            shift_one_grad,
            query_bias_grad,
            value_bias_grad,
            proj_bias_grad,
            gain_two_grad,
            shift_two_grad,
            up_bias_grad,
            down_bias_grad,
        ],
        axis=0,
    )
    qkv_sum, proj_sum, vector_sum = (
        lax.psum_scatter(qkv_grad.reshape(-1), ("dp", "seq"), scatter_dimension=0, tiled=True),
        lax.psum_scatter(proj_grad.reshape(-1), ("dp", "seq"), scatter_dimension=0, tiled=True),
        lax.psum_scatter(vector_grad, ("dp", "seq"), scatter_dimension=0, tiled=True),
    )
    return (block_output, input_grad, qkv_sum, proj_sum, up_sum, down_sum, vector_sum)


def pair_perm(size, mask):
    return [(number, number ^ mask) for number in range(size)]


def core_swap(value):
    return lax.ppermute(value, "seq", pair_perm(8, 1))


def chip_swap(value, mask):
    return lax.ppermute(value, "seq", pair_perm(8, 2 * mask))


def layer_swap(value, mask, layers):
    return lax.ppermute(value, "dp", pair_perm(layers, mask))


def put_blocks(pieces, index):
    stacked = jnp.zeros((len(pieces),) + pieces[0].shape, pieces[0].dtype)
    for mask, piece in enumerate(pieces):
        stacked = lax.dynamic_update_index_in_dim(stacked, piece, index ^ mask, 0)
    return stacked


def take_block(blocks, index):
    return lax.dynamic_index_in_dim(blocks, index, 0, keepdims=False)


def chip_gather(value):
    return [value] + [chip_swap(value, mask) for mask in (1, 2, 3)]


def layer_gather(value, layers):
    return [value] + [layer_swap(value, mask, layers) for mask in range(1, layers)]


def chip_deal(blocks, chip):
    return [take_block(blocks, chip)] + [
        chip_swap(take_block(blocks, chip ^ mask), mask) for mask in (1, 2, 3)
    ]


def chip_sum(blocks, chip):
    parts = chip_deal(blocks, chip)
    return (parts[0] + parts[1]) + (parts[2] + parts[3])


def layer_sum(blocks, layer, layers):
    total = take_block(blocks, layer)
    for mask in range(1, layers):
        total = total + layer_swap(take_block(blocks, layer ^ mask), mask, layers)
    return total


def core_sum(blocks, core):
    return take_block(blocks, core) + core_swap(take_block(blocks, 1 - core))


def spread_sum(value, layers):
    value = value + core_swap(value)
    value = value + chip_swap(value, 1) + chip_swap(value, 2) + chip_swap(value, 3)
    return value + sum(layer_swap(value, mask, layers) for mask in range(1, layers))


def local_fast(block_input, qkv_weight, proj_weight, up_weight, down_weight, vectors, out_grad):
    _, rows, width = block_input.shape
    layers = lax.axis_size("dp")
    hidden = down_weight.shape[0] * layers * 8 // width
    share = qkv_weight.shape[0] // (3 * width)
    hid_share = down_weight.shape[0] // width
    heads = H // 4
    head_size = width // H
    cols = heads * head_size
    hid_cols = hidden // 4
    layer = lax.axis_index("dp")
    place = lax.axis_index("seq")
    chip, core = place // 2, place % 2
    f32, bf16 = jnp.float32, jnp.bfloat16

    vec_own = jnp.zeros((layers * 8, vectors.shape[0]), bf16)
    vec_own = lax.dynamic_update_index_in_dim(vec_own, vectors, layer * 8 + place, 0)
    vec_all = spread_sum(vec_own, layers).reshape(-1).astype(f32)
    (gain1, shift1, query_bias, value_bias, proj_bias, gain2, shift2, up_bias, down_bias) = (
        split_vectors(vec_all, width, hidden)
    )
    query_bias = take_block(query_bias.reshape(4, cols), chip)
    value_bias = take_block(value_bias.reshape(4, cols), chip)
    up_bias = lax.dynamic_index_in_dim(
        up_bias.reshape(layers, 4, hidden // layers // 4), chip, 1, keepdims=False
    ).reshape(hid_cols)

    def own_sequence(value):
        kept = take_block(value, core)
        other = core_swap(take_block(value, 1 - core))
        return put_blocks([kept, other], core).reshape(2 * rows, width)

    def own_positions(value):
        blocks = value.reshape(2, rows, width)
        other = core_swap(take_block(blocks, 1 - core))
        return put_blocks([take_block(blocks, core), other], core)

    x_chip = own_sequence(block_input)
    x_all = put_blocks(chip_gather(x_chip), chip).reshape(8 * rows, width).astype(f32)
    g_chip = own_sequence(out_grad)
    g_all = jnp.concatenate(chip_gather(g_chip), axis=0)

    def gather_rows(blocks):
        mine = put_blocks(chip_deal(blocks, chip), chip)
        mine = put_blocks(layer_gather(mine, layers), layer)
        return jnp.moveaxis(put_blocks([mine, core_swap(mine)], core), 0, 2)

    qkv_blocks = qkv_weight.reshape(share, 3, 4, cols).transpose(2, 0, 1, 3).reshape(4, share, 3 * cols)
    mat_qkv = gather_rows(qkv_blocks).reshape(width, 3 * cols)
    up_blocks = (
        up_weight.reshape(share, layers, 4, hid_cols // layers)
        .transpose(2, 0, 1, 3)
        .reshape(4, share, hid_cols)
    )
    mat_up = gather_rows(up_blocks).reshape(width, hid_cols)
    down_own = put_blocks(
        layer_gather(down_weight.reshape(hid_share, width), layers), layer
    )
    mat_down = jnp.moveaxis(put_blocks([down_own, core_swap(down_own)], core), 0, 1).reshape(
        hid_cols, width
    )
    proj_own = put_blocks(layer_gather(proj_weight.reshape(share, width), layers), layer)
    proj_chip = put_blocks(chip_gather(proj_own), chip)
    mat_proj = (
        put_blocks([proj_chip, core_swap(proj_chip)], core)
        .transpose(2, 1, 0, 3, 4)
        .reshape(4, cols, width)
    )

    def dot(left, right):
        return jnp.dot(left, right, preferred_element_type=f32)

    def dot_nt(left, right):
        return lax.dot_general(left, right, (((1,), (1,)), ((), ())), preferred_element_type=f32)

    def dot_tn(left, right):
        return lax.dot_general(left, right, (((0,), (0,)), ((), ())), preferred_element_type=f32)

    act_one = layer_normalize(x_all, gain1, shift1)[0].astype(bf16)
    mixed = dot(act_one, mat_qkv)
    queries = (mixed[:, :cols] + query_bias).astype(bf16)
    keys = mixed[:, cols : 2 * cols].astype(bf16)
    values = (mixed[:, 2 * cols :] + value_bias).astype(bf16)
    length = 8 * rows
    scaling = head_size ** (-0.5)
    split = lambda value: value.reshape(length, heads, head_size)
    q3, k3, v3 = split(queries), split(keys), split(values)
    scores = jnp.einsum("qhd,khd->hqk", q3, k3, preferred_element_type=f32) * scaling
    row_pos = lax.broadcasted_iota(jnp.int32, (length, length), 0)
    col_pos = lax.broadcasted_iota(jnp.int32, (length, length), 1)
    scores = jnp.where((col_pos <= row_pos)[None], scores, masked_value)
    expo = jnp.exp(scores - jnp.max(scores, axis=-1, keepdims=True))
    probs = expo / jnp.sum(expo, axis=-1, keepdims=True)
    probs_low = probs.astype(bf16)
    attended = (
        jnp.einsum("hqk,khd->qhd", probs_low, v3, preferred_element_type=f32)
        .reshape(length, cols)
        .astype(bf16)
    )

    act_two = chip_deal(attended.reshape(4, 2 * rows, cols), chip)
    x_chip = x_chip.astype(f32)
    g_chip_f = g_chip.astype(f32)
    middle = x_chip + proj_bias
    for mask in range(4):
        middle = middle + dot(act_two[mask], take_block(mat_proj, chip ^ mask))
    second, second_normed, second_inverse = layer_normalize(middle, gain2, shift2)
    act_three = jnp.concatenate(chip_gather(second.astype(bf16)), axis=0)

    pre_act = dot(act_three, mat_up) + up_bias
    activated, slope = gelu_both(pre_act)
    act_four = activated.astype(bf16)
    grad_pre = (dot_nt(g_all, mat_down) * slope).astype(bf16)
    second_parts = dot_nt(grad_pre, mat_up).reshape(4, 2 * rows, width)
    out_parts = dot(act_four, mat_down).reshape(4, 2 * rows, width)

    def mask_sum(parts):
        return (parts[0] + chip_swap(parts[1], 1)) + (
            chip_swap(parts[2], 2) + chip_swap(parts[3], 3)
        )

    second_grad = mask_sum(second_parts)
    grad_mid_part, gain2_grad, shift2_grad = norm_back(
        second_grad, second_normed, second_inverse, gain2
    )
    grad_middle = g_chip_f + grad_mid_part
    grad_branch = grad_middle.astype(bf16)

    grad_att = put_blocks(
        [dot_nt(grad_branch, take_block(mat_proj, chip)).astype(bf16)]
        + [
            chip_swap(dot_nt(grad_branch, take_block(mat_proj, chip ^ mask)).astype(bf16), mask)
            for mask in (1, 2, 3)
        ],
        chip,
    ).reshape(length, cols)
    ga3 = split(grad_att)
    prob_grad = jnp.einsum("qhd,khd->hqk", ga3, v3, preferred_element_type=f32)
    score_grad = (
        probs * (prob_grad - jnp.sum(probs * prob_grad, axis=-1, keepdims=True))
    ).astype(bf16)
    grad_q = jnp.einsum("hqk,khd->qhd", score_grad, k3, preferred_element_type=f32) * scaling
    grad_k = jnp.einsum("hqk,qhd->khd", score_grad, q3, preferred_element_type=f32) * scaling
    grad_v = jnp.einsum("hqk,qhd->khd", probs_low, ga3, preferred_element_type=f32)
    grad_mixed = jnp.concatenate(
        [part.reshape(length, cols).astype(bf16) for part in (grad_q, grad_k, grad_v)], axis=1
    )
    first_parts = dot_nt(grad_mixed, mat_qkv).reshape(4, 2 * rows, width)
    first_grad = chip_sum(first_parts, chip)
    _, first_normed, first_inverse = layer_normalize(x_chip, gain1, shift1)
    grad_in_part, gain1_grad, shift1_grad = norm_back(
        first_grad, first_normed, first_inverse, gain1
    )
    input_grad = own_positions((grad_middle + grad_in_part).astype(bf16))
    block_output = own_positions((middle + mask_sum(out_parts) + down_bias).astype(bf16))

    def scatter_rows(grad):
        cut = jnp.moveaxis(grad.reshape(layers, 4, 2, share, grad.shape[1]), 2, 0)
        cut = layer_sum(core_sum(cut, core), layer, layers)
        return put_blocks(chip_deal(cut, chip), chip)

    up_sum = (
        scatter_rows(dot_tn(act_three, grad_pre))
        .reshape(4, share, layers, hid_cols // layers)
        .transpose(1, 2, 0, 3)
        .reshape(-1)
    )
    qkv_sum = (
        scatter_rows(dot_tn(act_one, grad_mixed))
        .reshape(4, share, 3, cols)
        .transpose(1, 2, 0, 3)
        .reshape(-1)
    )
    down_cut = jnp.moveaxis(
        dot_tn(act_four, g_all).reshape(layers, 2, hid_share, width), 1, 0
    )
    down_sum = layer_sum(core_sum(down_cut, core), layer, layers).reshape(-1)
    proj_rows = put_blocks([dot_tn(part, grad_branch) for part in act_two], chip)
    proj_cut = proj_rows.reshape(layers, 4, 2, share, width).transpose(2, 1, 0, 3, 4)
    proj_sum = layer_sum(chip_sum(core_sum(proj_cut, core), chip), layer, layers).reshape(-1)

    def in_place(value, index, count):
        return lax.dynamic_update_index_in_dim(
            jnp.zeros((count,) + value.shape, f32), value, index, 0
        )

    column_sum = lambda value: jnp.sum(value.astype(f32), axis=0)
    up_bias_grad = jnp.moveaxis(
        in_place(column_sum(grad_pre).reshape(layers, hid_cols // layers), chip, 4), 0, 1
    ).reshape(-1)
    vector_grad = jnp.concatenate(
        [
            gain1_grad,
            shift1_grad,
            in_place(column_sum(grad_mixed[:, :cols]), chip, 4).reshape(-1),
            in_place(column_sum(grad_mixed[:, 2 * cols :]), chip, 4).reshape(-1),
            column_sum(grad_branch),
            gain2_grad,
            shift2_grad,
            up_bias_grad,
            column_sum(g_chip_f),
        ]
    ).reshape(layers * 8, -1)
    vector_sum = take_block(spread_sum(vector_grad, layers), layer * 8 + place)
    return (block_output, input_grad, qkv_sum, proj_sum, up_sum, down_sum, vector_sum)


def solution(mesh):
    fast = mesh.shape["seq"] == 8 and mesh.shape["dp"] == 4
    return jax.shard_map(
        local_fast if fast else local,
        mesh=mesh,
        in_specs=(
            P("dp", "seq", None),
            P(("dp", "seq")),
            P(("dp", "seq")),
            P(("dp", "seq")),
            P(("dp", "seq")),
            P(("dp", "seq")),
            P("dp", "seq", None),
        ),
        out_specs=(
            P("dp", "seq", None),
            P("dp", "seq", None),
            P(("dp", "seq")),
            P(("dp", "seq")),
            P(("dp", "seq")),
            P(("dp", "seq")),
            P(("dp", "seq")),
        ),
        check_vma=False,
    )
```

```python
import jax
import jax.numpy as jnp
from jax import lax
from jax.experimental import pallas as pl
from jax.experimental.pallas import tpu as pltpu
from jax.sharding import PartitionSpec as P

H = 12


norm_eps = 1e-05
gelu_coeff = 0.7978845608028654
cubic_coeff = 0.044715
masked_value = -1e30


def layer_normalize(values, gain_vec, shift_vec):
    center = values - jnp.mean(values, axis=-1, keepdims=True)
    inverse = lax.rsqrt(jnp.mean(center * center, axis=-1, keepdims=True) + norm_eps)
    normed = center * inverse
    return (normed * gain_vec + shift_vec, normed, inverse)


def norm_back(grad_norm, normed, inverse, gain_vec):
    scaled = grad_norm * gain_vec
    inner_part = (
        scaled
        - jnp.mean(scaled, axis=-1, keepdims=True)
        - normed * jnp.mean(scaled * normed, axis=-1, keepdims=True)
    )
    return (inverse * inner_part, jnp.sum(grad_norm * normed, axis=0), jnp.sum(grad_norm, axis=0))


def gelu_both(pre_act):
    cubic = pre_act + cubic_coeff * pre_act * pre_act * pre_act
    tanh_part = jnp.tanh(gelu_coeff * cubic)
    value_now = 0.5 * pre_act * (1.0 + tanh_part)
    slope = 0.5 * (1.0 + tanh_part) + 0.5 * pre_act * (1.0 - tanh_part * tanh_part) * gelu_coeff * (
        1.0 + 3.0 * cubic_coeff * pre_act * pre_act
    )
    return (value_now, slope)


def split_vectors(vectors, model_width, hidden_width):
    offsets = [
        0,
        model_width,
        2 * model_width,
        3 * model_width,
        4 * model_width,
        5 * model_width,
        6 * model_width,
        7 * model_width,
        7 * model_width + hidden_width,
        8 * model_width + hidden_width,
    ]
    return tuple((vectors[offsets[number] : offsets[number + 1]] for number in range(9)))


def block_scores(queries, all_keys, all_values, key_index, key_block, first_query, scaling):
    start_row = key_index * key_block
    key_part = lax.dynamic_slice_in_dim(all_keys, start_row, key_block, 0)
    value_part = lax.dynamic_slice_in_dim(all_values, start_row, key_block, 0)
    raw_scores = (
        jnp.einsum("qhd,khd->hqk", queries, key_part, preferred_element_type=jnp.float32) * scaling
    )
    query_pos = first_query + lax.broadcasted_iota(jnp.int32, (queries.shape[0], key_block), 0)
    key_pos = start_row + lax.broadcasted_iota(jnp.int32, (queries.shape[0], key_block), 1)
    return (jnp.where((key_pos <= query_pos)[None], raw_scores, masked_value), key_part, value_part)


def attend(queries, all_keys, all_values, first_query):
    row_count, head_count, head_size = queries.shape
    key_block = min(512, all_keys.shape[0])
    scaling = head_size ** (-0.5)
    block_count = (first_query + row_count - 1) // key_block + 1

    def statistics(key_index, running):
        row_max, row_sum = running
        scores = block_scores(
            queries, all_keys, all_values, key_index, key_block, first_query, scaling
        )[0]
        new_max = jnp.maximum(row_max, jnp.max(scores, axis=-1))
        row_sum = row_sum * jnp.exp(row_max - new_max) + jnp.sum(
            jnp.exp(scores - new_max[:, :, None]), axis=-1
        )
        return (new_max, row_sum)

    starting = (
        jnp.full((head_count, row_count), masked_value, jnp.float32),
        jnp.zeros((head_count, row_count), jnp.float32),
    )
    row_max, row_sum = lax.fori_loop(0, block_count, statistics, starting)
    log_norm = row_max + jnp.log(row_sum)

    def accumulate(key_index, running):
        att_out, exact_out = running
        scores, key_part, value_part = block_scores(
            queries, all_keys, all_values, key_index, key_block, first_query, scaling
        )
        prob_exact = jnp.exp(scores - log_norm[:, :, None])
        prob_block = prob_exact.astype(jnp.bfloat16)
        att_out = att_out + jnp.einsum(
            "hqk,khd->qhd", prob_block, value_part, preferred_element_type=jnp.float32
        )
        exact_out = exact_out + jnp.einsum(
            "hqk,khd->qhd",
            prob_exact,
            value_part.astype(jnp.float32),
            precision=lax.Precision.HIGHEST,
            preferred_element_type=jnp.float32,
        )
        return (att_out, exact_out)

    zeros_out = jnp.zeros((row_count, head_count, head_size), jnp.float32)
    att_out, exact_out = lax.fori_loop(0, block_count, accumulate, (zeros_out, zeros_out))
    return (att_out, exact_out, log_norm)


def attend_back(queries, all_keys, all_values, first_query, grad_out, exact_out, log_norm):
    row_count, head_count, head_size = queries.shape
    key_block = min(512, all_keys.shape[0])
    scaling = head_size ** (-0.5)
    block_count = (first_query + row_count - 1) // key_block + 1
    row_dot = jnp.einsum("qhd,qhd->hq", grad_out.astype(jnp.float32), exact_out)

    def one_block(key_index, running):
        grad_query, grad_keys, grad_values = running
        scores, key_part, value_part = block_scores(
            queries, all_keys, all_values, key_index, key_block, first_query, scaling
        )
        prob_block = jnp.exp(scores - log_norm[:, :, None])
        value_grad = jnp.einsum(
            "hqk,qhd->khd",
            prob_block.astype(jnp.bfloat16),
            grad_out,
            preferred_element_type=jnp.float32,
        )
        prob_grad = jnp.einsum(
            "qhd,khd->hqk", grad_out, value_part, preferred_element_type=jnp.float32
        )
        score_grad = (prob_block * (prob_grad - row_dot[:, :, None])).astype(jnp.bfloat16)
        grad_query = (
            grad_query
            + jnp.einsum("hqk,khd->qhd", score_grad, key_part, preferred_element_type=jnp.float32)
            * scaling
        )
        key_grad = (
            jnp.einsum("hqk,qhd->khd", score_grad, queries, preferred_element_type=jnp.float32)
            * scaling
        )
        start_row = key_index * key_block
        grad_keys = lax.dynamic_update_slice_in_dim(grad_keys, key_grad, start_row, 0)
        grad_values = lax.dynamic_update_slice_in_dim(grad_values, value_grad, start_row, 0)
        return (grad_query, grad_keys, grad_values)

    starting = (
        jnp.zeros((row_count, head_count, head_size), jnp.float32),
        jnp.zeros(all_keys.shape, jnp.float32),
        jnp.zeros(all_values.shape, jnp.float32),
    )
    return lax.fori_loop(0, block_count, one_block, starting)


def local(block_input, qkv_weight, proj_weight, up_weight, down_weight, vectors, out_grad):
    seq_count, row_count, model_width = block_input.shape
    token_count = seq_count * row_count
    head_count = H
    head_size = model_width // head_count
    first_query = lax.axis_index("seq") * row_count
    gathered = (
        lax.all_gather(qkv_weight, ("dp", "seq"), axis=0, tiled=True),
        lax.all_gather(proj_weight, ("dp", "seq"), axis=0, tiled=True),
        lax.all_gather(up_weight, ("dp", "seq"), axis=0, tiled=True),
        lax.all_gather(down_weight, ("dp", "seq"), axis=0, tiled=True),
        lax.all_gather(vectors, ("dp", "seq"), axis=0, tiled=True),
    )
    hidden_width = gathered[2].shape[0] // model_width

    def unpack(pieces):
        return (
            pieces[0].reshape(model_width, 3 * model_width),
            pieces[1].reshape(model_width, model_width),
            pieces[2].reshape(model_width, hidden_width),
            pieces[3].reshape(hidden_width, model_width),
            split_vectors(pieces[4].astype(jnp.float32), model_width, hidden_width),
        )

    mat_qkv, mat_proj, mat_up, mat_down, vec_parts = unpack(gathered)
    (
        first_norm_gain,
        first_norm_bias,
        query_bias,
        value_bias,
        proj_bias,
        second_norm_gain,
        second_norm_bias,
        up_bias,
        down_bias,
    ) = vec_parts
    input_tokens = block_input.reshape(token_count, model_width).astype(jnp.float32)
    first_normed_rows, first_centered_scaled, first_inverse_deviation = layer_normalize(
        input_tokens, first_norm_gain, first_norm_bias
    )
    act_one = first_normed_rows.astype(jnp.bfloat16)
    mixed = jnp.dot(act_one, mat_qkv, preferred_element_type=jnp.float32)
    shape_four = (seq_count, row_count, head_count, head_size)
    q_four = (mixed[:, :model_width] + query_bias).astype(jnp.bfloat16).reshape(shape_four)
    k_four = mixed[:, model_width : 2 * model_width].astype(jnp.bfloat16).reshape(shape_four)
    v_four = (mixed[:, 2 * model_width :] + value_bias).astype(jnp.bfloat16).reshape(shape_four)

    def forward_one(running, element):
        query_seq, key_seq, value_seq = element
        all_keys, all_values = (
            lax.all_gather(key_seq, "seq", axis=0, tiled=True),
            lax.all_gather(value_seq, "seq", axis=0, tiled=True),
        )
        att_out, exact_out, log_norm = attend(query_seq, all_keys, all_values, first_query)
        return (running, (att_out, exact_out, log_norm))

    unused_fwd, (att_all, exact_all, norm_all) = lax.scan(
        forward_one, None, (q_four, k_four, v_four)
    )
    act_two = att_all.reshape(token_count, model_width).astype(jnp.bfloat16)
    residual_midpoint = (
        input_tokens + jnp.dot(act_two, mat_proj, preferred_element_type=jnp.float32) + proj_bias
    )
    second_normed_rows, second_centered_scaled, second_inverse_deviation = layer_normalize(
        residual_midpoint, second_norm_gain, second_norm_bias
    )
    act_three = second_normed_rows.astype(jnp.bfloat16)
    pre_act = jnp.dot(act_three, mat_up, preferred_element_type=jnp.float32) + up_bias
    activated, slope = gelu_both(pre_act)
    act_four = activated.astype(jnp.bfloat16)
    result = (
        residual_midpoint
        + jnp.dot(act_four, mat_down, preferred_element_type=jnp.float32)
        + down_bias
    )
    block_output = result.astype(jnp.bfloat16).reshape(seq_count, row_count, model_width)
    back_weights = unpack(
        (
            lax.all_gather(qkv_weight, ("dp", "seq"), axis=0, tiled=True),
            lax.all_gather(proj_weight, ("dp", "seq"), axis=0, tiled=True),
            lax.all_gather(up_weight, ("dp", "seq"), axis=0, tiled=True),
            lax.all_gather(down_weight, ("dp", "seq"), axis=0, tiled=True),
            lax.all_gather(vectors, ("dp", "seq"), axis=0, tiled=True),
        )
    )
    back_qkv, back_proj, back_up, back_down, back_vec = back_weights
    backward_first_gain = back_vec[0]
    backward_second_gain = back_vec[5]
    grad_top = out_grad.reshape(token_count, model_width)
    grad_top_f = grad_top.astype(jnp.float32)
    down_grad = jnp.dot(act_four.T, grad_top, preferred_element_type=jnp.float32)
    down_bias_grad = jnp.sum(grad_top_f, axis=0)
    grad_act = jnp.dot(grad_top, back_down.T, preferred_element_type=jnp.float32)
    grad_pre = (grad_act * slope).astype(jnp.bfloat16)
    up_grad = jnp.dot(act_three.T, grad_pre, preferred_element_type=jnp.float32)
    up_bias_grad = jnp.sum(grad_pre.astype(jnp.float32), axis=0)
    second_norm_gradient = jnp.dot(grad_pre, back_up.T, preferred_element_type=jnp.float32)
    grad_mid_part, gain_two_grad, shift_two_grad = norm_back(
        second_norm_gradient, second_centered_scaled, second_inverse_deviation, backward_second_gain
    )
    grad_middle = grad_top_f + grad_mid_part
    up_sum, down_sum = (
        lax.psum_scatter(up_grad.reshape(-1), ("dp", "seq"), scatter_dimension=0, tiled=True),
        lax.psum_scatter(down_grad.reshape(-1), ("dp", "seq"), scatter_dimension=0, tiled=True),
    )
    grad_branch = grad_middle.astype(jnp.bfloat16)
    proj_grad = jnp.dot(act_two.T, grad_branch, preferred_element_type=jnp.float32)
    proj_bias_grad = jnp.sum(grad_branch.astype(jnp.float32), axis=0)
    grad_att = jnp.dot(grad_branch, back_proj.T, preferred_element_type=jnp.float32).astype(
        jnp.bfloat16
    )

    def backward_one(running, element):
        query_seq, key_seq, value_seq, grad_seq, exact_seq, norm_seq = element
        all_keys, all_values = (
            lax.all_gather(key_seq, "seq", axis=0, tiled=True),
            lax.all_gather(value_seq, "seq", axis=0, tiled=True),
        )
        grad_query, grad_keys, grad_values = attend_back(
            query_seq, all_keys, all_values, first_query, grad_seq, exact_seq, norm_seq
        )
        key_part, value_part = (
            lax.psum_scatter(
                grad_keys.astype(jnp.bfloat16), "seq", scatter_dimension=0, tiled=True
            ).astype(jnp.float32),
            lax.psum_scatter(
                grad_values.astype(jnp.bfloat16), "seq", scatter_dimension=0, tiled=True
            ).astype(jnp.float32),
        )
        return (
            running,
            (
                grad_query.astype(jnp.bfloat16),
                key_part.astype(jnp.bfloat16),
                value_part.astype(jnp.bfloat16),
            ),
        )

    unused_back, (grad_q_four, grad_k_four, grad_v_four) = lax.scan(
        backward_one,
        None,
        (q_four, k_four, v_four, grad_att.reshape(shape_four), exact_all, norm_all),
    )
    grad_queries = grad_q_four.reshape(token_count, model_width)
    grad_values_all = grad_v_four.reshape(token_count, model_width)
    grad_mixed = jnp.concatenate(
        [grad_queries, grad_k_four.reshape(token_count, model_width), grad_values_all], axis=1
    )
    qkv_grad = jnp.dot(act_one.T, grad_mixed, preferred_element_type=jnp.float32)
    query_bias_grad = jnp.sum(grad_queries.astype(jnp.float32), axis=0)
    value_bias_grad = jnp.sum(grad_values_all.astype(jnp.float32), axis=0)
    first_norm_gradient = jnp.dot(grad_mixed, back_qkv.T, preferred_element_type=jnp.float32)
    grad_in_part, gain_one_grad, shift_one_grad = norm_back(
        first_norm_gradient, first_centered_scaled, first_inverse_deviation, backward_first_gain
    )
    input_grad = (
        (grad_middle + grad_in_part).astype(jnp.bfloat16).reshape(seq_count, row_count, model_width)
    )
    vector_grad = jnp.concatenate(
        [
            gain_one_grad,
            shift_one_grad,
            query_bias_grad,
            value_bias_grad,
            proj_bias_grad,
            gain_two_grad,
            shift_two_grad,
            up_bias_grad,
            down_bias_grad,
        ],
        axis=0,
    )
    qkv_sum, proj_sum, vector_sum = (
        lax.psum_scatter(qkv_grad.reshape(-1), ("dp", "seq"), scatter_dimension=0, tiled=True),
        lax.psum_scatter(proj_grad.reshape(-1), ("dp", "seq"), scatter_dimension=0, tiled=True),
        lax.psum_scatter(vector_grad, ("dp", "seq"), scatter_dimension=0, tiled=True),
    )
    return (block_output, input_grad, qkv_sum, proj_sum, up_sum, down_sum, vector_sum)


F32, BF16, F16 = jnp.float32, jnp.bfloat16, jnp.float16


def dot(left, right):
    return jnp.dot(left, right, preferred_element_type=F32)


def dot_nt(left, right):
    return lax.dot_general(left, right, (((1,), (1,)), ((), ())), preferred_element_type=F32)


def dot_tn(left, right):
    return lax.dot_general(left, right, (((0,), (0,)), ((), ())), preferred_element_type=F32)


def pair_perm(size, mask):
    return [(number, number ^ mask) for number in range(size)]


def core_swap(value):
    return lax.ppermute(value, "seq", pair_perm(8, 1))


def chip_swap(value, mask):
    return lax.ppermute(value, "seq", pair_perm(8, 2 * mask))


def layer_swap(value, mask):
    return lax.ppermute(value, "dp", pair_perm(4, mask))


def take_block(blocks, index):
    return lax.dynamic_index_in_dim(blocks, index, 0, keepdims=False)


def put_blocks(pieces, index):
    stacked = jnp.zeros((len(pieces),) + pieces[0].shape, pieces[0].dtype)
    for mask, piece in enumerate(pieces):
        stacked = lax.dynamic_update_index_in_dim(stacked, piece, index ^ mask, 0)
    return stacked


def core_sum(blocks, core):
    return take_block(blocks, core) + core_swap(take_block(blocks, 1 - core))


def chip_deal(blocks, chip):
    return [take_block(blocks, chip)] + [
        chip_swap(take_block(blocks, chip ^ mask), mask) for mask in (1, 2, 3)
    ]


def layer_sum(blocks, layer):
    total = take_block(blocks, layer)
    for mask in (1, 2, 3):
        total = total + layer_swap(take_block(blocks, layer ^ mask), mask)
    return total


def after(value, *others):
    return lax.optimization_barrier((value,) + others)[0]


def order_matrix(chip, core, share, count):
    natural = lax.broadcasted_iota(jnp.int32, (count, count), 0)
    position = lax.broadcasted_iota(jnp.int32, (1, count), 1)
    half = 4 * share
    core_mask = (position >= half).astype(jnp.int32)
    rest = position - core_mask * half
    chip_mask = sum((rest >= share * step).astype(jnp.int32) for step in (1, 2, 3))
    inner = rest - chip_mask * share
    wanted = ((chip ^ chip_mask) * 2 + (core ^ core_mask)) * share + inner
    return (natural == wanted).astype(F32).astype(BF16)


def restore_rows(own_ref, other_ref, out_ref, layer, order, half):
    for mask in range(4):
        block = jnp.concatenate([own_ref[mask, :half], other_ref[mask, :half]], axis=0)
        start = pl.multiple_of((layer ^ mask) * (2 * half), 2 * half)
        out_ref[pl.ds(start, 2 * half), :] = dot(order, block).astype(BF16)


def chip_lanes(row, chip, size):
    total = jnp.zeros((row.shape[0], size), F32)
    for number in range(4):
        total = total + jnp.where(chip == number, row[:, number * size : (number + 1) * size], 0.0)
    return total


def attend_kernel(index, x0, x1, x2, x3, own_w, other_w, vec, act, q3, k3, v3, lse, stat, out, mat, att):
    layer, chip, core = index[0], index[1], index[2]
    heads, length, size = q3.shape
    cols = heads * size
    block = length // 4
    half = 4 * (mat.shape[0] // 32)
    order = order_matrix(chip, core, half // 4, 2 * half)
    restore_rows(own_w, other_w, mat, layer, order, half)
    gain, shift = vec[0:1, :], vec[1:2, :]
    q_bias = chip_lanes(vec[2:3, :], chip, cols)
    v_bias = chip_lanes(vec[3:4, :], chip, cols)
    weight = mat[...]
    for mask, ref in enumerate((x0, x1, x2, x3)):
        rows = pl.ds(pl.multiple_of((chip ^ mask) * block, block), block)
        tokens = ref[...].astype(F32)
        mean = jnp.mean(tokens, axis=-1, keepdims=True)
        center = tokens - mean
        inverse = lax.rsqrt(jnp.mean(center * center, axis=-1, keepdims=True) + norm_eps)
        stat[rows, 0:1] = mean
        stat[rows, 1:2] = inverse
        act_one = (center * inverse * gain + shift).astype(BF16)
        act[rows, :] = act_one
        mixed = dot(act_one, weight)
        queries = (mixed[:, :cols] + q_bias).astype(BF16)
        keys = mixed[:, cols : 2 * cols].astype(BF16)
        values = (mixed[:, 2 * cols :] + v_bias).astype(BF16)
        for head in range(heads):
            lanes = slice(head * size, (head + 1) * size)
            q3[head, rows, :] = queries[:, lanes]
            k3[head, rows, :] = keys[:, lanes]
            v3[head, rows, :] = values[:, lanes]
    scaling = size ** (-0.5)
    below = lax.broadcasted_iota(jnp.int32, (block, block), 0) >= lax.broadcasted_iota(
        jnp.int32, (block, block), 1
    )

    def one_head(head, carry):
        for number in range(4):
            start, end = number * block, (number + 1) * block
            q_part = q3[head, start:end, :] * BF16(scaling)
            k_part = k3[head, :end, :]
            scores = dot_nt(q_part, k_part)
            last = jnp.where(below, scores[:, start:], masked_value)
            top = jnp.max(last, axis=-1, keepdims=True)
            if number:
                top = jnp.maximum(top, jnp.max(scores[:, :start], axis=-1, keepdims=True))
                scores = jnp.concatenate([scores[:, :start], last], axis=-1)
            else:
                scores = last
            expo = jnp.exp(scores - top)
            total = jnp.sum(expo, axis=-1, keepdims=True)
            probs_low = (expo * (1.0 / total)).astype(BF16)
            att[head, start:end, :] = dot(probs_low, v3[head, :end, :]).astype(BF16)
            lse[head, start:end, :] = top + jnp.log(total)
        return carry

    lax.fori_loop(0, heads, one_head, 0)
    for mask in range(4):
        rows = pl.ds(pl.multiple_of((chip ^ mask) * block, block), block)
        out[mask] = jnp.concatenate([att[head, rows, :] for head in range(heads)], axis=-1)


def project_kernel(index, p0, p1, p2, p3, own_w, other_w, x_ref, vec, middle, act, mat):
    layer, chip, core = index[0], index[1], index[2]
    cols = p0.shape[1]
    half = cols // 2
    order = order_matrix(chip, core, half // 4, cols)
    for mask in range(4):
        block = jnp.concatenate([own_w[mask], other_w[mask]], axis=0)
        mat[layer ^ mask] = dot(order, block).astype(BF16)
    total = x_ref[...].astype(F32)
    branch = jnp.zeros_like(total)
    for mask, ref in enumerate((p0, p1, p2, p3)):
        branch = branch + dot(ref[...], mat[chip ^ mask])
    total = total + (branch + vec[4:5, :])
    middle[...] = total
    center = total - jnp.mean(total, axis=-1, keepdims=True)
    inverse = lax.rsqrt(jnp.mean(center * center, axis=-1, keepdims=True) + norm_eps)
    act[...] = (center * inverse * vec[5:6, :] + vec[6:7, :]).astype(BF16)


def write_scaled(parts, peak, out):
    count, rows = out.shape[0], parts
    expo = jnp.floor(jnp.log2(jnp.maximum(peak, 1e-30)))
    factor = jnp.exp2(14.0 - expo)
    for number in range(count):
        out[number, :rows, :] = out[number, :rows, :] * factor
        out[number, rows:, :] = jnp.broadcast_to(expo, (out.shape[1] - rows, out.shape[2]))


def feed_kernel(
    index, a0, a1, a2, a3, g0, g1, g2, g3, own_u, other_u, own_d, other_d, vec,
    second, result, act_all, g_all, act_four, grad_pre, bias_grad, up, down,
):
    layer, chip, core = index[0], index[1], index[2]
    rows = a0.shape[0]
    hidden = down.shape[0]
    half = own_u.shape[1]
    order = order_matrix(chip, core, half // 4, 2 * half)
    restore_rows(own_u, other_u, up, layer, order, half)
    for mask in range(4):
        for core_mask, ref in enumerate((own_d, other_d)):
            start = pl.multiple_of(((layer ^ mask) * 2 + (core ^ core_mask)) * half, half)
            down[pl.ds(start, half), :] = ref[mask]
    piece = hidden // 4
    bias = jnp.concatenate(
        [chip_lanes(vec[7 + number : 8 + number, :], chip, piece) for number in range(4)], axis=-1
    )
    for number, (a_ref, g_ref) in enumerate(((a0, g0), (a1, g1), (a2, g2), (a3, g3))):
        act_all[number * rows : (number + 1) * rows, :] = a_ref[...]
        g_all[number * rows : (number + 1) * rows, :] = g_ref[...]
    bias_grad[...] = jnp.zeros_like(bias_grad)

    def one_block(number, peaks):
        span = pl.ds(pl.multiple_of(number * rows, rows), rows)
        pre_act = dot(act_all[span, :], up[...]) + bias
        activated, slope = gelu_both(pre_act)
        low = activated.astype(BF16)
        act_four[span, :] = low
        grad = (dot_nt(g_all[span, :], down[...]) * slope).astype(BF16)
        grad_pre[span, :] = grad
        bias_grad[...] += jnp.sum(grad.astype(F32), axis=0, keepdims=True)
        second_part = dot_nt(grad, up[...])
        second[number, :rows, :] = second_part
        result_part = dot(low, down[...])
        result[number, :rows, :] = result_part
        return (
            jnp.maximum(peaks[0], jnp.max(jnp.abs(second_part), keepdims=True)),
            jnp.maximum(peaks[1], jnp.max(jnp.abs(result_part), keepdims=True)),
        )

    zero = jnp.zeros((1, 1), F32)
    peaks = lax.fori_loop(0, 4, one_block, (zero, zero))
    write_scaled(rows, peaks[0], second)
    write_scaled(rows, peaks[1], result)


def attend_back_kernel(
    index, q3, k3, v3, lse, p0, p1, p2, p3, mat, x0, x1, x2, x3, stat,
    mixed, first, vec_grad, mix_grad, ga3, gq3, gk3, gv3, key_sum, value_sum,
):
    chip = index[1]
    heads, length, size = q3.shape
    block = length // 4
    scaling = size ** (-0.5)
    for mask, ref in enumerate((p0, p1, p2, p3)):
        rows = pl.ds(pl.multiple_of((chip ^ mask) * block, block), block)
        whole = ref[...]
        for head in range(heads):
            ga3[head, rows, :] = whole[:, head * size : (head + 1) * size]
    below = lax.broadcasted_iota(jnp.int32, (block, block), 0) >= lax.broadcasted_iota(
        jnp.int32, (block, block), 1
    )

    def one_head(head, carry):
        key_sum[...] = jnp.zeros_like(key_sum)
        value_sum[...] = jnp.zeros_like(value_sum)
        for number in range(4):
            start, end = number * block, (number + 1) * block
            q_part = q3[head, start:end, :] * BF16(scaling)
            k_part = k3[head, :end, :]
            grad = ga3[head, start:end, :]
            scores = dot_nt(q_part, k_part)
            last = jnp.where(below, scores[:, start:], masked_value)
            scores = jnp.concatenate([scores[:, :start], last], axis=-1) if number else last
            probs = jnp.exp(scores - lse[head, start:end, :])
            prob_grad = dot_nt(grad, v3[head, :end, :])
            row_dot = jnp.sum(probs * prob_grad, axis=-1, keepdims=True)
            score_grad = (probs * (prob_grad - row_dot)).astype(BF16)
            probs_low = probs.astype(BF16)
            gq3[head, start:end, :] = (dot(score_grad, k_part) * scaling).astype(BF16)
            key_sum[:end, :] += dot_tn(score_grad, q_part)
            value_sum[:end, :] += dot_tn(probs_low, grad)
        gk3[head] = key_sum[...].astype(BF16)
        gv3[head] = value_sum[...].astype(BF16)
        return carry

    lax.fori_loop(0, heads, one_head, 0)
    peak = jnp.zeros((1, 1), F32)
    vec_grad[...] = jnp.zeros_like(vec_grad)
    mix_grad[...] = jnp.zeros_like(mix_grad)
    for mask, ref in enumerate((x0, x1, x2, x3)):
        rows = pl.ds(pl.multiple_of((chip ^ mask) * block, block), block)
        whole = jnp.concatenate(
            [part[head, rows, :] for part in (gq3, gk3, gv3) for head in range(heads)], axis=-1
        )
        mixed[rows, :] = whole
        mix_grad[...] += jnp.sum(whole.astype(F32), axis=0, keepdims=True)
        part = dot_nt(whole, mat[...])
        first[mask, :block, :] = part
        peak = jnp.maximum(peak, jnp.max(jnp.abs(part), keepdims=True))
        normed = (ref[...].astype(F32) - stat[rows, 0:1]) * stat[rows, 1:2]
        vec_grad[0:1, :] += jnp.sum(part * normed, axis=0, keepdims=True)
        vec_grad[1:2, :] += jnp.sum(part, axis=0, keepdims=True)
    write_scaled(block, peak, first)


def call_kernel(body, name, outs, scratch, *args):
    shapes = tuple(jax.ShapeDtypeStruct(shape, kind) for shape, kind in outs)
    smem = pl.BlockSpec(memory_space=pltpu.SMEM)
    vmem = pl.BlockSpec(memory_space=pltpu.VMEM)
    return pl.pallas_call(
        body,
        name=name,
        out_shape=shapes,
        in_specs=[smem] + [vmem] * (len(args) - 1),
        out_specs=tuple(vmem for _ in outs),
        scratch_shapes=[pltpu.VMEM(shape, kind) for shape, kind in scratch],
        compiler_params=pltpu.CompilerParams(vmem_limit_bytes=48 * 1024 * 1024),
    )(*args)


def send_scaled(parts):
    rows = parts.shape[1] - 16

    def value_of(part):
        wide = part.astype(F32)
        return wide[:rows] * jnp.exp2(wide[rows : rows + 1, :1] - 14.0)

    own = parts[0, :rows] * jnp.exp2(parts[0, rows : rows + 1, :1] - 14.0)
    got = [chip_swap(parts[mask].astype(F16), mask) for mask in (1, 2, 3)]
    return (own + value_of(got[0])) + (value_of(got[1]) + value_of(got[2]))


def local_fast(block_input, qkv_weight, proj_weight, up_weight, down_weight, vectors, out_grad):
    _, rows, width = block_input.shape
    layers = 4
    share = qkv_weight.shape[0] // (3 * width)
    hid_share = down_weight.shape[0] // width
    heads = H // 4
    head_size = width // H
    cols = heads * head_size
    hid_cols = 8 * hid_share
    piece = hid_cols // layers
    hidden = 4 * hid_cols
    span = 2 * rows
    length = 4 * span
    vec_share = vectors.shape[0]
    layer = lax.axis_index("dp")
    place = lax.axis_index("seq")
    chip, core = place // 2, place % 2
    index = jnp.stack([layer, chip, core]).astype(jnp.int32)

    vec_lanes = 2 * width + 3 * cols
    message = jnp.concatenate(
        [
            up_weight.reshape(share, layers, 4, piece).transpose(2, 0, 1, 3).reshape(4, share, hid_cols),
            jnp.broadcast_to(proj_weight.reshape(1, share, width), (4, share, width)),
            qkv_weight.reshape(share, 3, 4, cols).transpose(2, 0, 1, 3).reshape(4, share, 3 * cols),
        ],
        axis=-1,
    )
    vec_row = jnp.pad(vectors.reshape(1, 1, vec_share), ((0, 0), (0, 7), (0, vec_lanes - vec_share)))
    message = jnp.concatenate([message, jnp.broadcast_to(vec_row, (4, 8, vec_lanes))], axis=1)
    dealt = chip_deal(message, chip)

    both = jnp.stack([block_input, out_grad])
    other = core_swap(lax.dynamic_index_in_dim(both, 1 - core, 1, keepdims=False))
    kept = lax.dynamic_index_in_dim(both, core, 1, keepdims=False)
    first_half = jnp.where(core == 0, kept, other)
    second_half = jnp.where(core == 0, other, kept)
    chip_tokens = jnp.concatenate([first_half, second_half], axis=1)
    x_chip, g_chip = chip_tokens[0], chip_tokens[1]
    x_all = [x_chip] + [chip_swap(x_chip, mask) for mask in (1, 2, 3)]

    def layers_of(value):
        mine = jnp.stack([value] + [layer_swap(value, mask) for mask in (1, 2, 3)])
        return mine, core_swap(mine)

    vec_rows = jnp.concatenate(
        [part[share : share + 1, : 3 * cols] for part in dealt]
        + [jnp.zeros((12, 3 * cols), BF16)],
        axis=0,
    )
    qkv_own, qkv_other = layers_of(
        jnp.concatenate([part[:share, 2 * width :] for part in dealt] + [vec_rows], axis=0)
    )
    proj_own, proj_other = layers_of(
        jnp.concatenate([part[:share, width : 2 * width] for part in dealt], axis=0)
    )
    feed_own, feed_other = layers_of(
        jnp.concatenate(
            [part[:share, :width] for part in dealt] + [down_weight.reshape(hid_share, width)], axis=0
        )
    )
    g_from = after(g_chip, *x_all[1:])
    g_all = [g_chip] + [chip_swap(g_from, mask) for mask in (1, 2, 3)]

    rows_at = 4 * share
    vec_parts = jnp.stack([qkv_own, qkv_other])[:, :, rows_at : rows_at + 4, :vec_share].reshape(
        32, vec_share
    )
    position = lax.broadcasted_iota(jnp.int32, (1, 32), 1)
    source = (
        (layer ^ ((position // 4) % 4)) * 8 + (chip ^ (position % 4)) * 2 + (core ^ (position // 16))
    )
    pick = (lax.broadcasted_iota(jnp.int32, (32, 32), 0) == source).astype(BF16)
    vec = dot(pick, vec_parts).reshape(-1, width)

    act_one, q3, k3, v3, lse, stat, att, mat_qkv = call_kernel(
        attend_kernel,
        "attend",
        [
            ((length, width), BF16),
            ((heads, length, head_size), BF16),
            ((heads, length, head_size), BF16),
            ((heads, length, head_size), BF16),
            ((heads, length, 1), F32),
            ((length, 2), F32),
            ((4, span, cols), BF16),
            ((width, 3 * cols), BF16),
        ],
        [((heads, length, head_size), BF16)],
        index, *x_all, qkv_own, qkv_other, vec,
    )
    act_two = [att[0]] + [chip_swap(att[mask], mask) for mask in (1, 2, 3)]
    middle, second_low, mat_proj = call_kernel(
        project_kernel,
        "project",
        [((span, width), F32), ((span, width), BF16), ((4, cols, width), BF16)],
        [],
        index, *act_two, proj_own, proj_other, x_chip, vec,
    )
    act_three = [second_low] + [chip_swap(second_low, mask) for mask in (1, 2, 3)]
    second_parts, out_parts, act_three, grad_top, act_four, grad_pre, up_bias_grad = call_kernel(
        feed_kernel,
        "feed",
        [
            ((4, span + 16, width), F32),
            ((4, span + 16, width), F32),
            ((length, width), BF16),
            ((length, width), BF16),
            ((length, hid_cols), BF16),
            ((length, hid_cols), BF16),
            ((1, hid_cols), F32),
        ],
        [((width, hid_cols), BF16), ((hid_cols, width), BF16)],
        index, *act_three, *g_all,
        feed_own[:, :rows_at], feed_other[:, :rows_at], feed_own[:, rows_at:], feed_other[:, rows_at:],
        vec,
    )

    second_grad = send_scaled(second_parts)
    gain1, gain2 = vec[0], vec[5]
    _, second_normed, second_inverse = layer_normalize(middle, gain2, vec[6])
    grad_mid_part, gain2_grad, shift2_grad = norm_back(
        second_grad, second_normed, second_inverse, gain2
    )
    g_chip_f = g_chip.astype(F32)
    grad_middle = g_chip_f + grad_mid_part
    grad_branch = grad_middle.astype(BF16)
    grad_att = [
        dot_nt(grad_branch, take_block(mat_proj, chip ^ mask)).astype(BF16) for mask in range(4)
    ]
    grad_att = [grad_att[0]] + [chip_swap(grad_att[mask], mask) for mask in (1, 2, 3)]
    grad_mixed, first_parts, norm_grads, mix_grad = call_kernel(
        attend_back_kernel,
        "attend_back",
        [
            ((length, 3 * cols), BF16),
            ((4, span + 16, width), F32),
            ((2, width), F32),
            ((1, 3 * cols), F32),
        ],
        [((heads, length, head_size), BF16)] * 4 + [((length, head_size), F32)] * 2,
        index, q3, k3, v3, lse, *grad_att, mat_qkv, *x_all, stat,
    )
    first_grad = send_scaled(first_parts)
    x_chip_f = x_chip.astype(F32)
    _, first_normed, first_inverse = layer_normalize(x_chip_f, gain1, vec[1])
    grad_in_part = norm_back(first_grad, first_normed, first_inverse, gain1)[0]
    in_grad = (grad_middle + grad_in_part).astype(BF16)
    out_parts = after(out_parts, second_grad)
    out_low = (middle + send_scaled(out_parts) + vec[11]).astype(BF16)

    results = jnp.stack([out_low, in_grad]).reshape(2, 2, rows, width)
    kept = lax.dynamic_index_in_dim(results, core, 1, keepdims=False)
    other = core_swap(lax.dynamic_index_in_dim(results, 1 - core, 1, keepdims=False))
    first_half = jnp.where(core == 0, kept, other)
    second_half = jnp.where(core == 0, other, kept)
    results = jnp.stack([first_half, second_half], axis=1)
    block_output, input_grad = results[0], results[1]

    def cut(grad):
        return jnp.moveaxis(grad.reshape(layers, 4, 2, share, grad.shape[1]), 2, 0)

    up_cut = cut(dot_tn(act_three, grad_pre))
    up_part = layer_sum(core_sum(up_cut, core), layer)
    down_cut = jnp.moveaxis(
        dot_tn(act_four, grad_top).reshape(layers, 2, hid_share, width), 1, 0
    )
    down_sum = layer_sum(core_sum(down_cut, core), layer).reshape(-1)
    proj_rows = put_blocks([dot_tn(part, grad_branch) for part in act_two], chip)
    proj_cut = proj_rows.reshape(layers, 4, 2, share, width).transpose(2, 1, 0, 3, 4)
    proj_parts = chip_deal(core_sum(proj_cut, core), chip)
    proj_sum = layer_sum((proj_parts[0] + proj_parts[1]) + (proj_parts[2] + proj_parts[3]), layer)
    qkv_part = layer_sum(core_sum(cut(dot_tn(act_one, grad_mixed)), core), layer)
    ready = put_blocks(chip_deal(jnp.concatenate([up_part, qkv_part], axis=-1), chip), chip)
    up_sum = (
        ready[:, :, :hid_cols].reshape(4, share, layers, piece).transpose(1, 2, 0, 3).reshape(-1)
    )
    qkv_sum = ready[:, :, hid_cols:].reshape(4, share, 3, cols).transpose(1, 2, 0, 3).reshape(-1)

    def in_place(value, count):
        return lax.dynamic_update_index_in_dim(
            jnp.zeros((count,) + value.shape, F32), value, chip, 0
        )

    up_bias_grad = jnp.moveaxis(in_place(up_bias_grad.reshape(layers, piece), 4), 0, 1).reshape(-1)
    vector_grad = jnp.concatenate(
        [
            norm_grads.reshape(-1),
            in_place(mix_grad[0, :cols], 4).reshape(-1),
            in_place(mix_grad[0, 2 * cols :], 4).reshape(-1),
            jnp.sum(grad_branch.astype(F32), axis=0),
            gain2_grad,
            shift2_grad,
            up_bias_grad,
            jnp.sum(g_chip_f, axis=0),
        ]
    )
    vec_cut = vector_grad.reshape(layers, 4, 2, vec_share).transpose(2, 1, 0, 3)
    vec_parts = chip_deal(core_sum(vec_cut, core), chip)
    vector_sum = layer_sum((vec_parts[0] + vec_parts[1]) + (vec_parts[2] + vec_parts[3]), layer)
    return (
        block_output,
        input_grad,
        qkv_sum,
        proj_sum.reshape(-1),
        up_sum,
        down_sum,
        vector_sum,
    )


def solution(mesh):
    fast = mesh.shape["seq"] == 8 and mesh.shape["dp"] == 4
    return jax.shard_map(
        local_fast if fast else local,
        mesh=mesh,
        in_specs=(
            P("dp", "seq", None),
            P(("dp", "seq")),
            P(("dp", "seq")),
            P(("dp", "seq")),
            P(("dp", "seq")),
            P(("dp", "seq")),
            P("dp", "seq", None),
        ),
        out_specs=(
            P("dp", "seq", None),
            P("dp", "seq", None),
            P(("dp", "seq")),
            P(("dp", "seq")),
            P(("dp", "seq")),
            P(("dp", "seq")),
            P(("dp", "seq")),
        ),
        check_vma=False,
    )
```
